128 devices in a mesh: region: 8 (over z, core), col: 16 (over x, y).
Axes of the slice: x: 4, y: 4, z: 4, core: 2. Of those that a mesh axis runs over, the one named last changes fastest.
Arguments:
- forcing: float32 [3, 512, 2048], P(None, 'region', 'col'), may hold values from 0.05 to 3
- river_storage: float32 [512, 2048], P('region', 'col'), may hold values from 0.1 to 4
- river_rate: float32 [512, 2048], P('region', 'col'), may hold values from 0.2 to 0.9
- flow_code: int32 [512, 2048], P('region', 'col'), may hold values from 1 to 128, as said below
- home_slot: int32 [128, 1024], P(('region', 'col')), may hold values from -1 to 1023, as said below
- home_offset: int32 [128, 1024], P(('region', 'col')), may hold values from 0 to 8184, as said below
- worker_list: int32 [61440], P(('region', 'col')), may hold values from 0 to 1023, as said below
- patch_cell: int32 [61440, 128], P(('region', 'col')), may hold values from 0 to 63, as said below
- patch_area: float32 [61440, 128], P(('region', 'col')), may hold values from 0.02 to 0.3
- canopy_water: float32 [61440, 128], P(('region', 'col')), may hold values from 0 to 1
- canopy_cap: float32 [61440, 128], P(('region', 'col')), may hold values from 0.1 to 2
- soil_water: float32 [15, 61440, 128], P(None, ('region', 'col')), may hold values from 0.05 to 0.5
- porosity: float32 [15, 61440, 128], P(None, ('region', 'col')), may hold values from 0.3 to 0.55
- drainage: float32 [15, 61440, 128], P(None, ('region', 'col')), may hold values from 0.02 to 0.8
Outputs:
- soil_new: float32 [15, 61440, 128], P(None, ('region', 'col'))
- canopy_new: float32 [61440, 128], P(('region', 'col'))
- cell_runoff: float32 [512, 2048], P('region', 'col')
- cell_evap: float32 [512, 2048], P('region', 'col')
- river_new: float32 [512, 2048], P('region', 'col')
The draws below stay inside these ranges and needn't reach their ends.
Inputs may be any that keep to these rules, and one draw needn't show every extreme that they name: `home_slot`: A home's live block slots come first and hold w * 8 + k (worker w, position k), distinct within the home; -1 marks unused slots. A home has 1024, 512, 256 or 128 live blocks, each for a quarter of the homes; at most 8 of one home's blocks go to one worker, and the busiest homes send exactly 8 to every worker. `worker_list`: every slot of every worker holds a live block; h * 8 + k at block b of worker w means home_slot[h, j] = w * 8 + k for exactly one j. `home_offset`: the first home cell of a live block, row-major over the home's cells; 0 for unused slots. Offset plus patch_cell stays below 8192. `patch_cell`: never falling along a block. `flow_code`: One-hot D8 codes as in the reference program.
All inputs are finite; a program needn't handle non-finite values.
Results may differ from the reference program's by a relative error of at most 0.000073.
Values sent between devices are 32-bit elements; how exact they have to be, the bound alone decides.
A program may use at most 64 MiB of HBM per device.

```python
import math
import jax
import jax.numpy as jnp
from jax import lax

LAYERS = 15
CR = 64
CC = 128
HB = 1024
ITERS = 4
CAP = 8
WB = 480
BLOCKS = 61440
NR = 512
NC = 2048
N_REGION = 8
N_COL = 16


def plan_tables(key):
    home_count = N_REGION * N_COL
    order = jax.random.permutation(jax.random.fold_in(key, 11), home_count).astype(jnp.int32)
    rank = jnp.zeros((home_count,), jnp.int32).at[order].set(jnp.arange(home_count, dtype=jnp.int32))
    rank = (rank - rank[home_count - 1] + home_count) % home_count
    divisor = jnp.array([1, 2, 4, 8], jnp.int32)[rank % 4]
    live_count = (HB // divisor).astype(jnp.int32)
    first = (jnp.cumsum(live_count) - live_count).astype(jnp.int32)
    slot_index = jnp.arange(HB, dtype=jnp.int32)[None, :]
    live_slot = slot_index < live_count[:, None]
    global_index = first[:, None] + slot_index
    worker = global_index % home_count
    worker_slot = global_index // home_count
    position = slot_index // home_count
    home_slot = jnp.where(live_slot, worker * CAP + position, -1).astype(jnp.int32)
    offset = jnp.where(live_slot, slot_index * (CR * CC) // live_count[:, None], 0).astype(jnp.int32)
    span_end = (slot_index + 1) * (CR * CC) // live_count[:, None]
    span = jnp.where(live_slot, span_end - offset, 1).astype(jnp.int32)
    target = jnp.where(live_slot, worker * WB + worker_slot, home_count * WB).reshape(-1)
    home_ids = jnp.broadcast_to(jnp.arange(home_count, dtype=jnp.int32)[:, None], (home_count, HB))
    worker_list = jnp.zeros((BLOCKS,), jnp.int32).at[target].set((home_ids * CAP + position).reshape(-1), mode='drop')
    block_span = jnp.ones((BLOCKS,), jnp.int32).at[target].set(span.reshape(-1), mode='drop')
    return (home_slot, offset, worker_list, block_span)


def draw_home_slot(key, part):
    return plan_tables(key)[0]


def draw_home_offset(key, part):
    return plan_tables(key)[1]


def draw_worker_list(key, part):
    return plan_tables(key)[2]


def draw_patch_cell(key, part):
    block_span = plan_tables(key)[3]
    coins = jax.random.randint(jax.random.fold_in(key, 23), (BLOCKS, 128), 0, 128)
    advance = (coins < block_span[:, None]).astype(jnp.int32)
    advance = advance.at[:, 0].set(0)
    cells = jnp.minimum(jnp.cumsum(advance, axis=1), block_span[:, None] - 1)
    cells = cells.at[:, 127].set(block_span - 1)
    return cells.astype(jnp.int32)


def draw_flow_code(key, part):
    powers = jax.random.randint(jax.random.fold_in(key, 31), (NR, NC), 0, 8)
    return jnp.left_shift(jnp.ones((NR, NC), jnp.int32), powers.astype(jnp.int32))


def block_scale(stream_key, extent, split, low, largest):
    def one(dim, blocks):
        steps = jax.random.uniform(jax.random.fold_in(jax.random.fold_in(stream_key, 6), dim), (blocks,), jnp.float32, low / len(split), largest / len(split))
        return jnp.repeat(jnp.exp(steps), extent[dim] // blocks).reshape((-1,) + (1,) * (len(extent) - dim - 1))

    gain = one(*split[0])
    for cut in split[1:]:
        gain = gain * one(*cut)
    return gain


def setup_inputs(seed: int = 0) -> dict:
    keys = jax.random.split(jax.random.key(seed), 15)
    forcing = jnp.clip(jnp.exp(math.log(3.0) - 4.0943445 * jax.random.uniform(keys[0], (3, NR, NC), jnp.float32) ** block_scale(keys[0], (3, NR, NC), ((1, 8), (2, 16)), -0.2, 0.2)), 0.05, 3.0)
    river_storage = jnp.clip(jnp.exp(math.log(4.0) - 3.6888794 * jax.random.uniform(keys[1], (NR, NC), jnp.float32) ** block_scale(keys[1], (NR, NC), ((0, 8), (1, 16)), -0.2, 0.2)), 0.1, 4.0)
    river_rate = jnp.clip(0.2 + 0.7 * jax.random.uniform(keys[2], (NR, NC), jnp.float32) ** block_scale(keys[2], (NR, NC), ((0, 8), (1, 16)), -0.2, 0.2), 0.2, 0.9)
    flow_code = draw_flow_code(jax.random.fold_in(keys[14], 71), 0)
    home_slot = draw_home_slot(jax.random.fold_in(keys[14], 71), 0)
    home_offset = draw_home_offset(jax.random.fold_in(keys[14], 71), 0)
    worker_list = draw_worker_list(jax.random.fold_in(keys[14], 71), 0)
    patch_cell = draw_patch_cell(jax.random.fold_in(keys[14], 71), 0)
    patch_area = jnp.clip(0.02 + 0.28 * jax.random.uniform(keys[8], (BLOCKS, 128), jnp.float32) ** block_scale(keys[8], (BLOCKS, 128), ((0, 128),), -0.2, 0.2), 0.02, 0.3)
    canopy_water = jnp.clip(1.0 * jax.random.uniform(keys[9], (BLOCKS, 128), jnp.float32) ** block_scale(keys[9], (BLOCKS, 128), ((0, 128),), -0.2, 0.2), 0.0, 1.0)
    canopy_cap = jnp.clip(jnp.exp(math.log(2.0) - 2.9957323 * jax.random.uniform(keys[10], (BLOCKS, 128), jnp.float32) ** block_scale(keys[10], (BLOCKS, 128), ((0, 128),), -0.2, 0.2)), 0.1, 2.0)
    soil_water = jnp.clip(0.05 + 0.45 * jax.random.uniform(keys[11], (LAYERS, BLOCKS, 128), jnp.float32) ** block_scale(keys[11], (LAYERS, BLOCKS, 128), ((1, 128),), -0.2, 0.2), 0.05, 0.5)
    porosity = jnp.clip(0.3 + 0.25 * jax.random.uniform(keys[12], (LAYERS, BLOCKS, 128), jnp.float32) ** block_scale(keys[12], (LAYERS, BLOCKS, 128), ((1, 128),), -0.2, 0.2), 0.3, 0.55)
    drainage = jnp.clip(jnp.exp(math.log(0.8) - 3.6888795 * jax.random.uniform(keys[13], (LAYERS, BLOCKS, 128), jnp.float32) ** block_scale(keys[13], (LAYERS, BLOCKS, 128), ((1, 128),), -0.2, 0.2)), 0.02, 0.8)
    return dict(forcing=forcing, river_storage=river_storage, river_rate=river_rate, flow_code=flow_code, home_slot=home_slot, home_offset=home_offset, worker_list=worker_list, patch_cell=patch_cell, patch_area=patch_area, canopy_water=canopy_water, canopy_cap=canopy_cap, soil_water=soil_water, porosity=porosity, drainage=drainage)


directions = ((0, 1), (1, 1), (1, 0), (1, -1), (0, -1), (-1, -1), (-1, 0), (-1, 1))


def inflow_from(out_pad, code_pad):
    inner_rows = out_pad.shape[0] - 2
    inner_cols = out_pad.shape[1] - 2
    arriving = jnp.zeros((inner_rows, inner_cols), jnp.float32)
    for code_bit, (row_step, col_step) in enumerate(directions):
        leaving_cell = jnp.where(code_pad == (1 << code_bit), out_pad, jnp.float32(0.0))
        arriving = arriving + leaving_cell[1 - row_step:1 - row_step + inner_rows, 1 - col_step:1 - col_step + inner_cols]
    return arriving


def layer_pass(state_in, layer_in):
    flowing, surface = state_in
    content, pore_room, drain_rate = layer_in
    filled = content + flowing
    excess = jnp.maximum(filled - pore_room, 0.0)
    filled = filled - excess
    drained = drain_rate * filled
    return (drained, surface + excess), filled - drained


def land_step(rainfall, demand, soil_demand, canopy_water, canopy_cap, soil_water, porosity, drainage):
    wetted = canopy_water + rainfall
    through = jnp.maximum(wetted - canopy_cap, 0.0)
    retained = jnp.minimum(wetted, canopy_cap)
    canopy_loss = jnp.minimum(demand, retained)
    canopy_new = retained - canopy_loss
    (bottom, surface), soil_mid = lax.scan(layer_pass, (through, jnp.zeros_like(through)), (soil_water, porosity, drainage))
    soil_loss = jnp.minimum(jnp.minimum(soil_demand, demand - canopy_loss), 0.5 * soil_mid[0])
    soil_new = soil_mid.at[0].add(-soil_loss)
    return canopy_new, soil_new, surface + bottom, canopy_loss + soil_loss


def reference(forcing, river_storage, river_rate, flow_code, home_slot, home_offset, worker_list, patch_cell, patch_area, canopy_water, canopy_cap, soil_water, porosity, drainage):
    home_count = N_REGION * N_COL
    cell_count = CR * CC
    source_home = worker_list // CAP
    position = worker_list % CAP
    worker_ids = jnp.arange(BLOCKS, dtype=jnp.int32) // WB
    pair_slot = worker_ids * CAP + position
    live_slot = home_slot >= 0
    home_rows = jnp.broadcast_to(jnp.arange(home_count, dtype=jnp.int32)[:, None], home_slot.shape)
    offset_table = jnp.zeros((home_count, HB), jnp.int32).at[home_rows, jnp.where(live_slot, home_slot, HB)].set(home_offset, mode="drop")
    block_offset = offset_table[source_home, pair_slot]
    patch_index = block_offset[:, None] + patch_cell
    home_of_patch = jnp.broadcast_to(source_home[:, None], patch_cell.shape)
    forcing_home = forcing.reshape(3, N_REGION, CR, N_COL, CC).transpose(0, 1, 3, 2, 4).reshape(3, home_count, cell_count)
    rainfall = forcing_home[0][home_of_patch, patch_index]
    demand = forcing_home[1][home_of_patch, patch_index]
    soil_demand = forcing_home[2][home_of_patch, patch_index]
    canopy_new, soil_new, runoff, transpired = land_step(rainfall, demand, soil_demand, canopy_water, canopy_cap, soil_water, porosity, drainage)
    runoff_home = jnp.zeros((home_count, cell_count), jnp.float32).at[home_of_patch, patch_index].add(patch_area * runoff)
    evap_home = jnp.zeros((home_count, cell_count), jnp.float32).at[home_of_patch, patch_index].add(patch_area * transpired)
    cell_runoff = runoff_home.reshape(N_REGION, N_COL, CR, CC).transpose(0, 2, 1, 3).reshape(NR, NC)
    cell_evap = evap_home.reshape(N_REGION, N_COL, CR, CC).transpose(0, 2, 1, 3).reshape(NR, NC)
    storage = river_storage + cell_runoff
    code_pad = jnp.pad(flow_code, 1)
    for sweep_index in range(ITERS):
        outflow = river_rate * storage
        storage = storage - outflow + inflow_from(jnp.pad(outflow, 1), code_pad)
    return soil_new, canopy_new, cell_runoff, cell_evap, storage
```

```python
import functools

import jax
import jax.numpy as jnp
from jax import lax
from jax.experimental import pallas as pl
from jax.experimental.pallas import tpu as pltpu
from jax.sharding import PartitionSpec as P

ITERS = 4
LANES = 128
SPAN = 64
ORDER = 37
CHUNK = 32
MESH = pl.DeviceIdType.MESH
f32, bf16, i32 = jnp.float32, jnp.bfloat16, jnp.int32


def iota(shape, dim):
    return lax.broadcasted_iota(i32, shape, dim)


def lane_take(values, index):
    numbers = lax.GatherDimensionNumbers(
        offset_dims=(),
        collapsed_slice_dims=(1,),
        start_index_map=(1,),
        operand_batching_dims=(0,),
        start_indices_batching_dims=(0,),
    )
    return lax.gather(
        values,
        index[..., None],
        numbers,
        slice_sizes=(1, 1),
        mode=lax.GatherScatterMode.PROMISE_IN_BOUNDS,
    )


def split3(value):
    high = value.astype(bf16)
    rest = value - high.astype(f32)
    middle = rest.astype(bf16)
    low = (rest - middle.astype(f32)).astype(bf16)
    return high, middle, low


def hot(mask):
    return jnp.where(mask, 1.0, 0.0).astype(bf16)


def dot(lhs, rhs):
    return lax.dot_general(
        lhs, rhs, (((1,), (0,)), ((), ())), preferred_element_type=f32
    )


def dot_nt(lhs, rhs):
    return lax.dot_general(
        lhs, rhs, (((1,), (1,)), ((), ())), preferred_element_type=f32
    )


def step_shift(step, n_row, n_col):
    code = (step * ORDER) % (n_row * n_col)
    return code // n_col, code % n_col


def locate_slots(me_r, me_c, n_row, n_col, slot, offset, rows, lanes):
    slots = slot.shape[1]
    part = 2 * LANES
    weight = jnp.where(
        iota((part, slots), 0) < LANES,
        lax.shift_right_logical(offset, 7),
        offset & (LANES - 1),
    )
    weight = weight.astype(f32).astype(bf16)
    for first in range(0, slots, part):
        index = iota((part, LANES), 0) + first
        step = lax.shift_right_logical(index, 3)
        code = (step * ORDER) & (n_row * n_col - 1)
        shift_r = lax.shift_right_logical(code, n_col.bit_length() - 1)
        shift_c = code & (n_col - 1)
        worker = ((me_r + shift_r) & (n_row - 1)) * n_col + ((me_c + shift_c) & (n_col - 1))
        wanted = worker * 8 + (index & 7)
        pick = jnp.concatenate(
            [hot(slot[:, l : l + LANES] == wanted) for l in range(0, slots, LANES)], axis=1
        )
        place = dot_nt(pick, weight)
        rows[first : first + part, :] = place[:, :LANES]
        lanes[first : first + part, :] = place[:, LANES:].astype(i32)


def cut_windows(forcing, rows, lanes, weight, windows):
    grid_rows = forcing.shape[1]
    for v in range(3):
        field = forcing[v]
        below = pltpu.roll(field, grid_rows - 1, 0)
        for d, (a, b) in enumerate(zip(split3(field), split3(below))):
            at = slice(d * grid_rows, (d + 1) * grid_rows)
            weight[at, v * LANES : (v + 1) * LANES] = a
            weight[at, (3 + v) * LANES : (4 + v) * LANES] = b
    weight[3 * grid_rows :, :] = jnp.zeros((4 * LANES // 2 - 3 * grid_rows, 6 * LANES), bf16)
    part = 2 * LANES
    lane = iota((part, LANES), 1)
    for first in range(0, rows.shape[0], part):
        at = slice(first, first + part)
        pick = hot(rows[at, :] == (lane & (grid_rows - 1)).astype(f32))
        both = dot(jnp.concatenate([pick, pick], axis=1), weight[...])
        start = lanes[at, :]
        index = ((lane & (SPAN - 1)) + start) & (LANES - 1)
        cut = []
        for v in range(3):
            near = both[:, v * LANES : (v + 1) * LANES]
            far = both[:, (3 + v) * LANES : (4 + v) * LANES]
            cut.append(lane_take(jnp.where(lane >= start, near, far), index))
        left = lane < SPAN
        pair = jnp.where(left, cut[0], cut[1])
        last = jnp.where(left, cut[2], pltpu.roll(cut[2], part - 4, 0))
        steps = slice(first // 8, (first + part) // 8)
        windows[steps, 0:8, :] = pair.reshape(part // 8, 8, LANES)
        windows[steps, 8:12, :] = last.reshape(part // 8, 8, LANES)[:, 0:4, :]


def block_pickers(listed, pick_rows, pick_slots):
    blocks = listed.shape[1]
    slots = pick_slots.shape[0]
    part = 2 * LANES
    for first in range(0, slots, part):
        row = iota((part, blocks), 0) + first
        pick_slots[first : first + part, :] = hot(row == listed)
    for first in range(0, blocks, LANES):
        size = min(LANES, blocks - first)
        column = jnp.broadcast_to(listed[:, first : first + size], (LANES, size)).T
        for l in range(0, slots, LANES):
            pick_rows[first : first + size, l : l + LANES] = hot(
                column == iota((size, LANES), 1) + l
            )


def segment_tables(at, cells, last_of, run):
    cell = cells[at, :]
    lane = iota(cell.shape, 1)
    wanted = lane & (SPAN - 1)
    place = jnp.zeros_like(lane)
    for step in (64, 32, 16, 8, 4, 2, 1):
        tried = place + step
        place = jnp.where(lane_take(cell, tried) <= wanted, tried, place)
    found = lane_take(cell, place) == wanted
    last_of[at, :] = jnp.where(found, place, place + LANES)
    start = jnp.where((lane == 0) | (pltpu.roll(cell, 1, 1) != cell), lane, 0)
    for step in (1, 2, 4, 8, 16, 32, 64):
        start = jnp.maximum(start, jnp.where(lane >= step, pltpu.roll(start, step, 1), 0))
    run[at, :] = lane - start


def gather_rows(arrived, pick_rows, parts, found):
    homes = arrived.shape[0]
    part = 2 * LANES
    for first in range(0, homes * 8, part):
        steps = slice(first // 8, (first + part) // 8)
        pair = arrived[steps, 0:8, :].reshape(part, LANES)
        half = arrived[steps, 8:12, :]
        last = jnp.concatenate([half, pltpu.roll(half, SPAN, 2)], axis=1).reshape(part, LANES)
        for d, (a, b) in enumerate(zip(split3(pair), split3(last))):
            parts[d, first : first + part, :LANES] = a
            parts[d, first : first + part, LANES:] = b
    pick = pick_rows[...]
    found[...] = dot(pick, parts[0]) + (dot(pick, parts[1]) + dot(pick, parts[2]))


def land_rows(
    at, found, cells, last_of, run, area, canopy_water, canopy_cap, canopy_out, soil, porosity, drainage, sums
):
    layers = soil.shape[0]
    cell = cells[at, :]
    lane = iota(cell.shape, 1)
    pair = found[at, :LANES]
    rainfall = lane_take(pair, cell)
    demand = lane_take(pair, cell + SPAN)
    soil_demand = lane_take(found[at, LANES:], cell)
    wetted = canopy_water[at, :] + rainfall
    cap = canopy_cap[at, :]
    flowing = jnp.maximum(wetted - cap, 0.0)
    retained = jnp.minimum(wetted, cap)
    canopy_loss = jnp.minimum(demand, retained)
    canopy_out[at, :] = retained - canopy_loss
    surface = jnp.zeros_like(flowing)
    transpired = canopy_loss
    for l in range(layers):
        filled = soil[l, at, :] + flowing
        excess = jnp.maximum(filled - porosity[l, at, :], 0.0)
        surface = surface + excess
        filled = filled - excess
        flowing = drainage[l, at, :] * filled
        kept = filled - flowing
        if l == 0:
            soil_loss = jnp.minimum(jnp.minimum(soil_demand, demand - canopy_loss), 0.5 * kept)
            kept = kept - soil_loss
            transpired = canopy_loss + soil_loss
        soil[l, at, :] = kept
    weight = area[at, :]
    runoff = weight * (surface + flowing)
    evap = weight * transpired
    before = run[at, :]
    for step in (1, 2, 4, 8, 16, 32, 64):
        same = before >= step
        runoff = runoff + jnp.where(same, pltpu.roll(runoff, step, 1), 0.0)
        evap = evap + jnp.where(same, pltpu.roll(evap, step, 1), 0.0)
    place = last_of[at, :]
    index = place & (LANES - 1)
    total = jnp.where(lane < SPAN, lane_take(runoff, index), lane_take(evap, index))
    total = jnp.where(place < LANES, total, 0.0)
    for d, piece in enumerate(split3(total)):
        sums[at, d * LANES : (d + 1) * LANES] = piece


def return_rows(pick_slots, sums, leaving):
    part = 2 * LANES
    for first in range(0, pick_slots.shape[0], part):
        three = dot(pick_slots[first : first + part, :], sums[...])
        total = three[:, :LANES] + (three[:, LANES : 2 * LANES] + three[:, 2 * LANES :])
        leaving[first // 8 : (first + part) // 8, :, :] = total.reshape(part // 8, 8, LANES)


def home_picker(rows, pick_cells):
    grid_rows = pick_cells.shape[0]
    for first in range(0, rows.shape[0], LANES):
        across = rows[first : first + LANES, :].T[:grid_rows, :]
        pick_cells[:, first : first + LANES] = hot(
            across == iota((grid_rows, LANES), 0).astype(f32)
        )


def place_sums(back, lanes, pick_cells):
    part = 2 * LANES
    grid_rows = pick_cells.shape[0]
    lane = iota((part, LANES), 1)
    total = jnp.zeros((grid_rows, 4 * LANES), f32)
    for first in range(0, pick_cells.shape[1], part):
        at = slice(first, first + part)
        sent = back[first // 8 : (first + part) // 8, :, :].reshape(part, LANES)
        start = lanes[at, :]
        index = (lane - start) & (LANES - 1)
        inside = index < SPAN
        near = inside & (lane >= start)
        far = inside & (lane < start)
        runoff = lane_take(sent, index)
        evap = lane_take(sent, (index + SPAN) & (LANES - 1))
        spread = jnp.concatenate(
            [
                jnp.where(near, runoff, 0.0),
                jnp.where(near, evap, 0.0),
                jnp.where(far, runoff, 0.0),
                jnp.where(far, evap, 0.0),
            ],
            axis=1,
        )
        high, middle, low = split3(spread)
        pick = pick_cells[:, at]
        total = total + (dot(pick, high) + (dot(pick, middle) + dot(pick, low)))
    first_row = iota((grid_rows, 2 * LANES), 0) == 0
    carried = pltpu.roll(total[:, 2 * LANES :], 1, 0)
    total = total[:, : 2 * LANES] + jnp.where(first_row, 0.0, carried)
    return total[:, :LANES], total[:, LANES:]


def pack_edges(field):
    lane = iota((8, LANES), 1)
    packed = jnp.zeros((8, LANES), field.dtype)
    for i in range(field.shape[0] // 8):
        piece = field[8 * i : 8 * i + 8, :]
        first = pltpu.roll(piece, 4 * i, 1) if i else piece
        last = pltpu.roll(piece, (SPAN + 4 * i + 4) % LANES, 1)
        packed = jnp.where((lane >= 4 * i) & (lane < 4 * i + 4), first, packed)
        packed = jnp.where((lane >= SPAN + 4 * i) & (lane < SPAN + 4 * i + 4), last, packed)
    return packed


def extend(field, halo, inside):
    up, down, left, right = inside
    lane = iota((8, LANES), 1)
    on_right = (lane < 4) & right
    on_left = (lane >= LANES - 4) & left

    def side(from_right, from_left):
        return jnp.where(on_right, from_right, jnp.where(on_left, from_left, 0.0))

    centre = jnp.concatenate(
        [jnp.where(up, halo[0], 0.0), field, jnp.where(down, halo[1], 0.0)], axis=0
    )
    sides = [jnp.where(up, side(halo[5], halo[4]), 0.0)]
    for i in range(field.shape[0] // 8):
        from_right = pltpu.roll(halo[3], LANES - 4 * i, 1) if i else halo[3]
        from_left = pltpu.roll(halo[2], LANES - 4 - (SPAN + 4 * i), 1) if 4 * i < SPAN - 4 else halo[2]
        sides.append(side(from_right, from_left))
    sides.append(jnp.where(down, side(halo[7], halo[6]), 0.0))
    return centre, jnp.concatenate(sides, axis=0)


def route(storage, rate, code):
    height = storage[0].shape[0]
    lane = iota(storage[0].shape, 1)

    def across(pair, east):
        centre, side = (pltpu.roll(x, 1 if east else LANES - 1, 1) for x in pair)
        edge = lane == (0 if east else LANES - 1)
        return jnp.where(edge, side, centre), jnp.where(edge, centre, side)

    def inflow(outflow):
        def from_row(step, column):
            bits = {
                (0, 1): 1, (1, 1): 2, (1, 0): 4, (1, -1): 8,
                (0, -1): 16, (-1, -1): 32, (-1, 0): 64, (-1, 1): 128,
            }
            if (step, column) == (0, 0):
                return None
            bit = float(bits[step, column])
            return [jnp.where(c == bit, o, 0.0) for c, o in zip(code, outflow)]

        total = None
        for column in (1, 0, -1):
            gathered = None
            for step in (1, -1, 0):
                moved = from_row(step, column)
                if moved is None:
                    continue
                if step:
                    moved = [pltpu.roll(x, 1 if step > 0 else height - 1, 0) for x in moved]
                gathered = moved if gathered is None else [a + b for a, b in zip(gathered, moved)]
            if column:
                gathered = across(gathered, column > 0)
            total = list(gathered) if total is None else [a + b for a, b in zip(total, gathered)]
        return total

    for _ in range(ITERS):
        outflow = [a * b for a, b in zip(rate, storage)]
        storage = [s - o + n for s, o, n in zip(storage, outflow, inflow(outflow))]
    return storage[0]


def step_kernel(
    n_row,
    n_col,
    forcing_h, storage_h, rate_h, code_h, slot_h, offset_h, list_h,
    cell_h, area_h, water_h, cap_h, soil_h, porosity_h, drainage_h,
    soil_o, canopy_o, runoff_o, evap_o, river_o,
    forcing, storage, rate, code, slot, offset, listed,
    cells, area, water, cap, canopy, soil, porosity, drainage,
    rows, lanes, weight, windows, arrived, pick_rows, pick_slots, pick_cells,
    last_of, run, parts, found, sums, leaving, back,
    fixed_edge, fixed_halo, edge, halo,
    load_sem, store_sem, fixed_sem, edge_sem, out_sem, back_sem,
):
    me_r, me_c = lax.axis_index("region"), lax.axis_index("col")
    me = me_r * n_col + me_c
    devices = n_row * n_col

    def peer(step, sign):
        shift_r, shift_c = step_shift(step, n_row, n_col)
        if sign > 0:
            return (me_r + shift_r) % n_row, (me_c + shift_c) % n_col
        return (me_r + n_row - shift_r) % n_row, (me_c + n_col - shift_c) % n_col

    barrier = pltpu.get_barrier_semaphore()

    def greet(step, carry):
        pl.semaphore_signal(barrier, inc=1, device_id=peer(step, 1), device_id_type=MESH)
        return carry

    lax.fori_loop(1, devices, greet, 0)

    loads = [
        (slot_h, slot), (offset_h, offset), (forcing_h, forcing), (rate_h, rate), (code_h, code),
        (list_h, listed), (cell_h, cells), (storage_h, storage), (area_h, area),
        (water_h, water), (cap_h, cap), (soil_h, soil), (porosity_h, porosity), (drainage_h, drainage),
    ]
    loads = [pltpu.make_async_copy(a, b, load_sem.at[i]) for i, (a, b) in enumerate(loads)]
    for copy in loads:
        copy.start()
    for copy in loads[:3]:
        copy.wait()
    locate_slots(me_r, me_c, n_row, n_col, slot[...], offset[...], rows, lanes)
    cut_windows(forcing, rows, lanes, weight, windows)

    pl.semaphore_wait(barrier, devices - 1)

    def send_out(step, carry):
        pltpu.make_async_remote_copy(
            src_ref=windows.at[step], dst_ref=arrived.at[me],
            send_sem=out_sem.at[0], recv_sem=out_sem.at[1],
            device_id=peer(step, 1), device_id_type=MESH,
        ).start()
        return carry

    lax.fori_loop(1, devices, send_out, 0)
    arrived[me] = windows[0]

    def neighbour(down, right):
        return (me_r + n_row + down) % n_row, (me_c + n_col + right) % n_col

    routes = [
        (2, (1, 0)), (1, (-1, 0)), (0, (0, 1)), (0, (0, -1)),
        (2, (1, 1)), (2, (1, -1)), (1, (-1, 1)), (1, (-1, -1)),
    ]

    def edge_copies(source, target, sems):
        return [
            pltpu.make_async_remote_copy(
                src_ref=source.at[which], dst_ref=target.at[i],
                send_sem=sems.at[0, i], recv_sem=sems.at[1, i],
                device_id=neighbour(*to), device_id_type=MESH,
            )
            for i, (which, to) in enumerate(routes)
        ]

    loads[3].wait()
    loads[4].wait()
    height = rate.shape[0]
    for first, field in ((0, rate[...]), (8, code[...].astype(f32))):
        at = slice(first, first + 8)
        fixed_edge[0, at, :] = pack_edges(field)
        fixed_edge[1, at, :] = field[:8, :]
        fixed_edge[2, at, :] = field[height - 8 :, :]
    fixed_copies = edge_copies(fixed_edge, fixed_halo, fixed_sem)
    for copy in fixed_copies:
        copy.start()

    loads[5].wait()
    block_pickers(listed[...], pick_rows, pick_slots)
    home_picker(rows, pick_cells)
    loads[6].wait()
    blocks = cells.shape[0]

    def chunk(i):
        return pl.ds(pl.multiple_of(i * CHUNK, CHUNK), CHUNK)

    def tables(i, carry):
        segment_tables(chunk(i), cells, last_of, run)
        return carry

    lax.fori_loop(0, blocks // CHUNK, tables, 0)
    for copy in loads[7:]:
        copy.wait()

    most = pl.ds(0, devices - 1)
    pltpu.make_async_copy(arrived.at[most], arrived.at[most], out_sem.at[1]).wait()
    gather_rows(arrived, pick_rows, parts, found)

    def land(i, carry):
        land_rows(
            chunk(i), found, cells, last_of, run, area, water, cap, canopy, soil, porosity, drainage, sums
        )
        return carry

    lax.fori_loop(0, blocks // CHUNK, land, 0)
    return_rows(pick_slots, sums, leaving)

    def send_back(step, carry):
        to_r, to_c = peer(step, -1)
        pltpu.make_async_remote_copy(
            src_ref=leaving.at[to_r * n_col + to_c], dst_ref=back.at[step],
            send_sem=back_sem.at[0], recv_sem=back_sem.at[1],
            device_id=(to_r, to_c), device_id_type=MESH,
        ).start()
        return carry

    lax.fori_loop(1, devices, send_back, 0)
    back[0] = leaving[me]
    stores = [
        pltpu.make_async_copy(soil, soil_o, store_sem.at[0]),
        pltpu.make_async_copy(canopy, canopy_o, store_sem.at[1]),
    ]
    for copy in stores:
        copy.start()
    for copy in fixed_copies:
        copy.wait()
    pltpu.make_async_copy(windows.at[most], windows.at[most], out_sem.at[0]).wait()

    inside = (me_r > 0, me_r < n_row - 1, me_c > 0, me_c < n_col - 1)
    pltpu.make_async_copy(back.at[most], back.at[most], back_sem.at[1]).wait()
    cell_runoff, cell_evap = place_sums(back, lanes, pick_cells)
    runoff_o[...] = cell_runoff
    evap_o[...] = cell_evap
    river = storage[...] + cell_runoff
    edge[0] = pack_edges(river)
    edge[1] = river[:8, :]
    edge[2] = river[height - 8 :, :]
    edge_sent = edge_copies(edge, halo, edge_sem)
    for copy in edge_sent:
        copy.start()
    whole_rate = extend(rate[...], [fixed_halo[i, 0:8, :] for i in range(8)], inside)
    whole_code = extend(code[...].astype(f32), [fixed_halo[i, 8:16, :] for i in range(8)], inside)
    for copy in edge_sent:
        copy.wait()
    whole = extend(river, [halo[i] for i in range(8)], inside)
    final = route(whole, whole_rate, whole_code)
    river_o[...] = final[8 : 8 + height, :]
    pltpu.make_async_copy(leaving.at[most], leaving.at[most], back_sem.at[0]).wait()
    for copy in stores:
        copy.wait()


def shards(
    forcing, river_storage, river_rate, flow_code, home_slot, home_offset, worker_list,
    patch_cell, patch_area, canopy_water, canopy_cap, soil_water, porosity, drainage,
):
    n_row, n_col = lax.axis_size("region"), lax.axis_size("col")
    devices = n_row * n_col
    grid = river_storage.shape
    slots = home_slot.shape[1]
    blocks = patch_cell.shape[0]
    layers = soil_water.shape[0]
    listed = worker_list.reshape(1, blocks)
    vmem = pltpu.VMEM
    dma = pltpu.SemaphoreType.DMA
    patch = (blocks, LANES)
    scratch = [
        vmem(forcing.shape, f32), vmem(grid, f32), vmem(grid, f32), vmem(grid, i32),
        vmem((1, slots), i32), vmem((1, slots), i32), vmem((1, blocks), i32),
        vmem(patch, i32), vmem(patch, f32), vmem(patch, f32), vmem(patch, f32), vmem(patch, f32),
        vmem((layers,) + patch, f32), vmem((layers,) + patch, f32), vmem((layers,) + patch, f32),
        vmem((slots, LANES), f32), vmem((slots, LANES), i32),
        vmem((2 * LANES, 6 * LANES), bf16),
        vmem((devices, 12, LANES), f32), vmem((devices, 12, LANES), f32),
        vmem((blocks, slots), bf16), vmem((slots, blocks), bf16), vmem((grid[0], slots), bf16),
        vmem(patch, i32), vmem(patch, i32),
        vmem((3, slots, 2 * LANES), bf16), vmem((blocks, 2 * LANES), f32),
        vmem((blocks, 3 * LANES), bf16),
        vmem((devices, 8, LANES), f32), vmem((devices, 8, LANES), f32),
        vmem((3, 16, LANES), f32), vmem((8, 16, LANES), f32),
        vmem((3, 8, LANES), f32), vmem((8, 8, LANES), f32),
        dma((14,)), dma((2,)), dma((2, 8)), dma((2, 8)), dma((2,)), dma((2,)),
    ]
    hbm = pl.BlockSpec(memory_space=pl.ANY)
    near = pl.BlockSpec(memory_space=pltpu.VMEM)
    return pl.pallas_call(
        functools.partial(step_kernel, n_row, n_col),
        out_shape=(
            jax.ShapeDtypeStruct(soil_water.shape, f32),
            jax.ShapeDtypeStruct(patch, f32),
            jax.ShapeDtypeStruct(grid, f32),
            jax.ShapeDtypeStruct(grid, f32),
            jax.ShapeDtypeStruct(grid, f32),
        ),
        in_specs=[hbm] * 14,
        out_specs=(hbm, hbm, near, near, near),
        scratch_shapes=scratch,
        compiler_params=pltpu.CompilerParams(
            collective_id=0, has_side_effects=True, vmem_limit_bytes=56 * 1024 * 1024
        ),
        name="land_step",
    )(
        forcing, river_storage, river_rate, flow_code, home_slot, home_offset, listed,
        patch_cell, patch_area, canopy_water, canopy_cap, soil_water, porosity, drainage,
    )


def solution(mesh):
    both = ("region", "col")
    grid = P("region", "col")
    return jax.shard_map(
        shards,
        mesh=mesh,
        in_specs=(
            P(None, "region", "col"), grid, grid, grid,
            P(both, None), P(both, None), P(both),
            P(both, None), P(both, None), P(both, None), P(both, None),
            P(None, both, None), P(None, both, None), P(None, both, None),
        ),
        out_specs=(P(None, both, None), P(both, None), grid, grid, grid),
        check_vma=False,
    )
```

```python
import functools

import jax
import jax.numpy as jnp
from jax import lax
from jax.experimental import pallas as pl
from jax.experimental.pallas import tpu as pltpu
from jax.sharding import PartitionSpec as P

ITERS = 4
LANES = 128
SPAN = 64
ORDER = 37
CHUNK = 32
MESH = pl.DeviceIdType.MESH
f32, bf16, i32 = jnp.float32, jnp.bfloat16, jnp.int32


def iota(shape, dim):
    return lax.broadcasted_iota(i32, shape, dim)


def lane_take(values, index):
    numbers = lax.GatherDimensionNumbers(
        offset_dims=(),
        collapsed_slice_dims=(1,),
        start_index_map=(1,),
        operand_batching_dims=(0,),
        start_indices_batching_dims=(0,),
    )
    return lax.gather(
        values,
        index[..., None],
        numbers,
        slice_sizes=(1, 1),
        mode=lax.GatherScatterMode.PROMISE_IN_BOUNDS,
    )


def split3(value):
    high = value.astype(bf16)
    rest = value - high.astype(f32)
    middle = rest.astype(bf16)
    low = (rest - middle.astype(f32)).astype(bf16)
    return high, middle, low


def hot(mask):
    return jnp.where(mask, 1.0, 0.0).astype(bf16)


def dot(lhs, rhs):
    return lax.dot_general(
        lhs, rhs, (((1,), (0,)), ((), ())), preferred_element_type=f32
    )


def dot_nt(lhs, rhs):
    return lax.dot_general(
        lhs, rhs, (((1,), (1,)), ((), ())), preferred_element_type=f32
    )


def step_shift(step, n_row, n_col):
    code = (step * ORDER) % (n_row * n_col)
    return code // n_col, code % n_col


def locate_slots(me_r, me_c, n_row, n_col, slot, offset, rows, lanes):
    slots = slot.shape[1]
    part = 2 * LANES
    weight = jnp.where(
        iota((part, slots), 0) < LANES,
        lax.shift_right_logical(offset, 7),
        offset & (LANES - 1),
    )
    weight = weight.astype(f32).astype(bf16)
    for first in range(0, slots, part):
        index = iota((part, LANES), 0) + first
        step = lax.shift_right_logical(index, 3)
        code = (step * ORDER) & (n_row * n_col - 1)
        shift_r = lax.shift_right_logical(code, n_col.bit_length() - 1)
        shift_c = code & (n_col - 1)
        worker = ((me_r + shift_r) & (n_row - 1)) * n_col + ((me_c + shift_c) & (n_col - 1))
        wanted = worker * 8 + (index & 7)
        pick = jnp.concatenate(
            [hot(slot[:, l : l + LANES] == wanted) for l in range(0, slots, LANES)], axis=1
        )
        place = dot_nt(pick, weight)
        rows[first : first + part, :] = place[:, :LANES]
        lanes[first : first + part, :] = place[:, LANES:].astype(i32)


def cut_windows(forcing, rows, lanes, weight, windows):
    grid_rows = forcing.shape[1]
    for v in range(3):
        field = forcing[v]
        below = pltpu.roll(field, grid_rows - 1, 0)
        for d, (a, b) in enumerate(zip(split3(field), split3(below))):
            at = slice(d * grid_rows, (d + 1) * grid_rows)
            weight[at, v * LANES : (v + 1) * LANES] = a
            weight[at, (3 + v) * LANES : (4 + v) * LANES] = b
    weight[3 * grid_rows :, :] = jnp.zeros((4 * LANES // 2 - 3 * grid_rows, 6 * LANES), bf16)
    part = 2 * LANES
    lane = iota((part, LANES), 1)
    for first in range(0, rows.shape[0], part):
        at = slice(first, first + part)
        pick = hot(rows[at, :] == (lane & (grid_rows - 1)).astype(f32))
        both = dot(jnp.concatenate([pick, pick], axis=1), weight[...])
        start = lanes[at, :]
        index = ((lane & (SPAN - 1)) + start) & (LANES - 1)
        cut = []
        for v in range(3):
            near = both[:, v * LANES : (v + 1) * LANES]
            far = both[:, (3 + v) * LANES : (4 + v) * LANES]
            cut.append(lane_take(jnp.where(lane >= start, near, far), index))
        left = lane < SPAN
        pair = jnp.where(left, cut[0], cut[1])
        last = jnp.where(left, cut[2], pltpu.roll(cut[2], part - 4, 0))
        steps = slice(first // 8, (first + part) // 8)
        windows[steps, 0:8, :] = pair.reshape(part // 8, 8, LANES)
        windows[steps, 8:12, :] = last.reshape(part // 8, 8, LANES)[:, 0:4, :]


def block_pickers(listed, pick_rows, pick_slots):
    blocks = listed.shape[1]
    slots = pick_slots.shape[0]
    part = 2 * LANES
    for first in range(0, slots, part):
        row = iota((part, blocks), 0) + first
        pick_slots[first : first + part, :] = hot(row == listed)
    for first in range(0, blocks, LANES):
        size = min(LANES, blocks - first)
        column = jnp.broadcast_to(listed[:, first : first + size], (LANES, size)).T
        for l in range(0, slots, LANES):
            pick_rows[first : first + size, l : l + LANES] = hot(
                column == iota((size, LANES), 1) + l
            )


def segment_tables(at, cells, last_of, run):
    cell = cells[at, :]
    lane = iota(cell.shape, 1)
    wanted = lane & (SPAN - 1)
    place = jnp.zeros_like(lane)
    for step in (64, 32, 16, 8, 4, 2, 1):
        tried = place + step
        place = jnp.where(lane_take(cell, tried) <= wanted, tried, place)
    found = lane_take(cell, place) == wanted
    last_of[at, :] = jnp.where(found, place, place + LANES)
    start = jnp.where((lane == 0) | (pltpu.roll(cell, 1, 1) != cell), lane, 0)
    for step in (1, 2, 4, 8, 16, 32, 64):
        start = jnp.maximum(start, jnp.where(lane >= step, pltpu.roll(start, step, 1), 0))
    run[at, :] = lane - start


def gather_rows(arrived, pick_rows, parts, found):
    homes = arrived.shape[0]
    part = 2 * LANES
    for first in range(0, homes * 8, part):
        steps = slice(first // 8, (first + part) // 8)
        pair = arrived[steps, 0:8, :].reshape(part, LANES)
        half = arrived[steps, 8:12, :]
        last = jnp.concatenate([half, pltpu.roll(half, SPAN, 2)], axis=1).reshape(part, LANES)
        for d, (a, b) in enumerate(zip(split3(pair), split3(last))):
            parts[d, first : first + part, :LANES] = a
            parts[d, first : first + part, LANES:] = b
    pick = pick_rows[...]
    found[...] = dot(pick, parts[0]) + (dot(pick, parts[1]) + dot(pick, parts[2]))


def land_rows(
    at, found, cells, last_of, run, area, canopy_water, canopy_cap, canopy_out, soil, porosity, drainage, sums
):
    layers = soil.shape[0]
    cell = cells[at, :]
    lane = iota(cell.shape, 1)
    pair = found[at, :LANES]
    rainfall = lane_take(pair, cell)
    demand = lane_take(pair, cell + SPAN)
    soil_demand = lane_take(found[at, LANES:], cell)
    wetted = canopy_water[at, :] + rainfall
    cap = canopy_cap[at, :]
    flowing = jnp.maximum(wetted - cap, 0.0)
    retained = jnp.minimum(wetted, cap)
    canopy_loss = jnp.minimum(demand, retained)
    canopy_out[at, :] = retained - canopy_loss
    surface = jnp.zeros_like(flowing)
    transpired = canopy_loss
    for l in range(layers):
        filled = soil[l, at, :] + flowing
        excess = jnp.maximum(filled - porosity[l, at, :], 0.0)
        surface = surface + excess
        filled = filled - excess
        flowing = drainage[l, at, :] * filled
        kept = filled - flowing
        if l == 0:
            soil_loss = jnp.minimum(jnp.minimum(soil_demand, demand - canopy_loss), 0.5 * kept)
            kept = kept - soil_loss
            transpired = canopy_loss + soil_loss
        soil[l, at, :] = kept
    weight = area[at, :]
    runoff = weight * (surface + flowing)
    evap = weight * transpired
    before = run[at, :]
    for step in (1, 2, 4, 8, 16, 32, 64):
        same = before >= step
        runoff = runoff + jnp.where(same, pltpu.roll(runoff, step, 1), 0.0)
        evap = evap + jnp.where(same, pltpu.roll(evap, step, 1), 0.0)
    place = last_of[at, :]
    index = place & (LANES - 1)
    total = jnp.where(lane < SPAN, lane_take(runoff, index), lane_take(evap, index))
    total = jnp.where(place < LANES, total, 0.0)
    for d, piece in enumerate(split3(total)):
        sums[at, d * LANES : (d + 1) * LANES] = piece


def return_rows(pick_slots, sums, leaving):
    part = 2 * LANES
    for first in range(0, pick_slots.shape[0], part):
        three = dot(pick_slots[first : first + part, :], sums[...])
        total = three[:, :LANES] + (three[:, LANES : 2 * LANES] + three[:, 2 * LANES :])
        leaving[first // 8 : (first + part) // 8, :, :] = total.reshape(part // 8, 8, LANES)


def home_picker(rows, pick_cells):
    grid_rows = pick_cells.shape[0]
    for first in range(0, rows.shape[0], LANES):
        across = rows[first : first + LANES, :].T[:grid_rows, :]
        pick_cells[:, first : first + LANES] = hot(
            across == iota((grid_rows, LANES), 0).astype(f32)
        )


def place_sums(back, lanes, pick_cells):
    part = 2 * LANES
    grid_rows = pick_cells.shape[0]
    lane = iota((part, LANES), 1)
    total = jnp.zeros((grid_rows, 4 * LANES), f32)
    for first in range(0, pick_cells.shape[1], part):
        at = slice(first, first + part)
        sent = back[first // 8 : (first + part) // 8, :, :].reshape(part, LANES)
        start = lanes[at, :]
        index = (lane - start) & (LANES - 1)
        inside = index < SPAN
        near = inside & (lane >= start)
        far = inside & (lane < start)
        runoff = lane_take(sent, index)
        evap = lane_take(sent, (index + SPAN) & (LANES - 1))
        spread = jnp.concatenate(
            [
                jnp.where(near, runoff, 0.0),
                jnp.where(near, evap, 0.0),
                jnp.where(far, runoff, 0.0),
                jnp.where(far, evap, 0.0),
            ],
            axis=1,
        )
        high, middle, low = split3(spread)
        pick = pick_cells[:, at]
        total = total + (dot(pick, high) + (dot(pick, middle) + dot(pick, low)))
    first_row = iota((grid_rows, 2 * LANES), 0) == 0
    carried = pltpu.roll(total[:, 2 * LANES :], 1, 0)
    total = total[:, : 2 * LANES] + jnp.where(first_row, 0.0, carried)
    return total[:, :LANES], total[:, LANES:]


def pack_edges(field):
    lane = iota((8, LANES), 1)
    packed = jnp.zeros((8, LANES), field.dtype)
    for i in range(field.shape[0] // 8):
        piece = field[8 * i : 8 * i + 8, :]
        first = pltpu.roll(piece, 4 * i, 1) if i else piece
        last = pltpu.roll(piece, (SPAN + 4 * i + 4) % LANES, 1)
        packed = jnp.where((lane >= 4 * i) & (lane < 4 * i + 4), first, packed)
        packed = jnp.where((lane >= SPAN + 4 * i) & (lane < SPAN + 4 * i + 4), last, packed)
    return packed


def extend(field, halo, inside):
    up, down, left, right = inside
    lane = iota((8, LANES), 1)
    on_right = (lane < 4) & right
    on_left = (lane >= LANES - 4) & left

    def side(from_right, from_left):
        return jnp.where(on_right, from_right, jnp.where(on_left, from_left, 0.0))

    centre = jnp.concatenate(
        [jnp.where(up, halo[0], 0.0), field, jnp.where(down, halo[1], 0.0)], axis=0
    )
    sides = [jnp.where(up, side(halo[5], halo[4]), 0.0)]
    for i in range(field.shape[0] // 8):
        from_right = pltpu.roll(halo[3], LANES - 4 * i, 1) if i else halo[3]
        from_left = pltpu.roll(halo[2], LANES - 4 - (SPAN + 4 * i), 1) if 4 * i < SPAN - 4 else halo[2]
        sides.append(side(from_right, from_left))
    sides.append(jnp.where(down, side(halo[7], halo[6]), 0.0))
    return centre, jnp.concatenate(sides, axis=0)


def route(storage, rate, code):
    height = storage[0].shape[0]
    lane = iota(storage[0].shape, 1)

    def across(pair, east):
        centre, side = (pltpu.roll(x, 1 if east else LANES - 1, 1) for x in pair)
        edge = lane == (0 if east else LANES - 1)
        return jnp.where(edge, side, centre), jnp.where(edge, centre, side)

    def inflow(outflow):
        def from_row(step, column):
            bits = {
                (0, 1): 1, (1, 1): 2, (1, 0): 4, (1, -1): 8,
                (0, -1): 16, (-1, -1): 32, (-1, 0): 64, (-1, 1): 128,
            }
            if (step, column) == (0, 0):
                return None
            bit = float(bits[step, column])
            return [jnp.where(c == bit, o, 0.0) for c, o in zip(code, outflow)]

        total = None
        for column in (1, 0, -1):
            gathered = None
            for step in (1, -1, 0):
                moved = from_row(step, column)
                if moved is None:
                    continue
                if step:
                    moved = [pltpu.roll(x, 1 if step > 0 else height - 1, 0) for x in moved]
                gathered = moved if gathered is None else [a + b for a, b in zip(gathered, moved)]
            if column:
                gathered = across(gathered, column > 0)
            total = list(gathered) if total is None else [a + b for a, b in zip(total, gathered)]
        return total

    for _ in range(ITERS):
        outflow = [a * b for a, b in zip(rate, storage)]
        storage = [s - o + n for s, o, n in zip(storage, outflow, inflow(outflow))]
    return storage[0]


def step_kernel(
    n_row,
    n_col,
    forcing_h, storage_h, rate_h, code_h, slot_h, offset_h, list_h,
    cell_h, area_h, water_h, cap_h, soil_h, porosity_h, drainage_h,
    soil, canopy, runoff_o, evap_o, river_o,
    forcing, storage, rate, code, slot, offset, listed,
    cells, area, water, cap, porosity, drainage,
    rows, lanes, weight, windows, arrived, pick_rows, pick_slots, pick_cells,
    last_of, run, parts, found, sums, leaving, back,
    fixed_edge, fixed_halo, edge, halo,
    load_sem, fixed_sem, edge_sem, out_sem, back_sem,
):
    me_r, me_c = lax.axis_index("region"), lax.axis_index("col")
    me = me_r * n_col + me_c
    devices = n_row * n_col

    def peer(step, sign):
        shift_r, shift_c = step_shift(step, n_row, n_col)
        if sign > 0:
            return (me_r + shift_r) % n_row, (me_c + shift_c) % n_col
        return (me_r + n_row - shift_r) % n_row, (me_c + n_col - shift_c) % n_col

    barrier = pltpu.get_barrier_semaphore()

    def greet(step, carry):
        pl.semaphore_signal(barrier, inc=1, device_id=peer(step, 1), device_id_type=MESH)
        return carry

    lax.fori_loop(1, devices, greet, 0)

    loads = [
        (slot_h, slot), (offset_h, offset), (forcing_h, forcing), (rate_h, rate), (code_h, code),
        (list_h, listed), (cell_h, cells), (storage_h, storage), (area_h, area),
        (water_h, water), (cap_h, cap), (soil_h, soil), (porosity_h, porosity), (drainage_h, drainage),
    ]
    loads = [pltpu.make_async_copy(a, b, load_sem.at[i]) for i, (a, b) in enumerate(loads)]
    for copy in loads:
        copy.start()
    for copy in loads[:3]:
        copy.wait()
    locate_slots(me_r, me_c, n_row, n_col, slot[...], offset[...], rows, lanes)
    cut_windows(forcing, rows, lanes, weight, windows)

    pl.semaphore_wait(barrier, devices - 1)

    def send_out(step, carry):
        pltpu.make_async_remote_copy(
            src_ref=windows.at[step], dst_ref=arrived.at[me],
            send_sem=out_sem.at[0], recv_sem=out_sem.at[1],
            device_id=peer(step, 1), device_id_type=MESH,
        ).start()
        return carry

    lax.fori_loop(1, devices, send_out, 0)
    arrived[me] = windows[0]

    def neighbour(down, right):
        return (me_r + n_row + down) % n_row, (me_c + n_col + right) % n_col

    routes = [
        (2, (1, 0)), (1, (-1, 0)), (0, (0, 1)), (0, (0, -1)),
        (2, (1, 1)), (2, (1, -1)), (1, (-1, 1)), (1, (-1, -1)),
    ]

    def edge_copies(source, target, sems):
        return [
            pltpu.make_async_remote_copy(
                src_ref=source.at[which], dst_ref=target.at[i],
                send_sem=sems.at[0, i], recv_sem=sems.at[1, i],
                device_id=neighbour(*to), device_id_type=MESH,
            )
            for i, (which, to) in enumerate(routes)
        ]

    loads[3].wait()
    loads[4].wait()
    height = rate.shape[0]
    for first, field in ((0, rate[...]), (8, code[...].astype(f32))):
        at = slice(first, first + 8)
        fixed_edge[0, at, :] = pack_edges(field)
        fixed_edge[1, at, :] = field[:8, :]
        fixed_edge[2, at, :] = field[height - 8 :, :]
    fixed_copies = edge_copies(fixed_edge, fixed_halo, fixed_sem)
    for copy in fixed_copies:
        copy.start()

    loads[5].wait()
    block_pickers(listed[...], pick_rows, pick_slots)
    home_picker(rows, pick_cells)
    loads[6].wait()
    blocks = cells.shape[0]

    def chunk(i):
        return pl.ds(pl.multiple_of(i * CHUNK, CHUNK), CHUNK)

    def tables(i, carry):
        segment_tables(chunk(i), cells, last_of, run)
        return carry

    lax.fori_loop(0, blocks // CHUNK, tables, 0)
    for copy in loads[7:]:
        copy.wait()

    most = pl.ds(0, devices - 1)
    pltpu.make_async_copy(arrived.at[most], arrived.at[most], out_sem.at[1]).wait()
    gather_rows(arrived, pick_rows, parts, found)

    def land(i, carry):
        land_rows(
            chunk(i), found, cells, last_of, run, area, water, cap, canopy, soil, porosity, drainage, sums
        )
        return carry

    lax.fori_loop(0, blocks // CHUNK, land, 0)
    return_rows(pick_slots, sums, leaving)

    def send_back(step, carry):
        to_r, to_c = peer(step, -1)
        pltpu.make_async_remote_copy(
            src_ref=leaving.at[to_r * n_col + to_c], dst_ref=back.at[step],
            send_sem=back_sem.at[0], recv_sem=back_sem.at[1],
            device_id=(to_r, to_c), device_id_type=MESH,
        ).start()
        return carry

    lax.fori_loop(1, devices, send_back, 0)
    back[0] = leaving[me]
    for copy in fixed_copies:
        copy.wait()
    pltpu.make_async_copy(windows.at[most], windows.at[most], out_sem.at[0]).wait()

    inside = (me_r > 0, me_r < n_row - 1, me_c > 0, me_c < n_col - 1)
    pltpu.make_async_copy(back.at[most], back.at[most], back_sem.at[1]).wait()
    cell_runoff, cell_evap = place_sums(back, lanes, pick_cells)
    runoff_o[...] = cell_runoff
    evap_o[...] = cell_evap
    river = storage[...] + cell_runoff
    edge[0] = pack_edges(river)
    edge[1] = river[:8, :]
    edge[2] = river[height - 8 :, :]
    edge_sent = edge_copies(edge, halo, edge_sem)
    for copy in edge_sent:
        copy.start()
    whole_rate = extend(rate[...], [fixed_halo[i, 0:8, :] for i in range(8)], inside)
    whole_code = extend(code[...].astype(f32), [fixed_halo[i, 8:16, :] for i in range(8)], inside)
    for copy in edge_sent:
        copy.wait()
    whole = extend(river, [halo[i] for i in range(8)], inside)
    final = route(whole, whole_rate, whole_code)
    river_o[...] = final[8 : 8 + height, :]
    pltpu.make_async_copy(leaving.at[most], leaving.at[most], back_sem.at[0]).wait()


def store_kernel(*refs):
    count = (len(refs) - 1) // 2
    sources, targets, sems = refs[:count], refs[count : 2 * count], refs[-1]
    pairs = [(sources[0].at[l], targets[0].at[l]) for l in range(sources[0].shape[0])]
    pairs += list(zip(sources[1:], targets[1:]))
    copies = [pltpu.make_async_copy(a, b, sems.at[i]) for i, (a, b) in enumerate(pairs)]
    for copy in copies:
        copy.start()
    for copy in copies:
        copy.wait()


def shards(
    forcing, river_storage, river_rate, flow_code, home_slot, home_offset, worker_list,
    patch_cell, patch_area, canopy_water, canopy_cap, soil_water, porosity, drainage,
):
    n_row, n_col = lax.axis_size("region"), lax.axis_size("col")
    devices = n_row * n_col
    grid = river_storage.shape
    slots = home_slot.shape[1]
    blocks = patch_cell.shape[0]
    layers = soil_water.shape[0]
    listed = worker_list.reshape(1, blocks)
    vmem = pltpu.VMEM
    dma = pltpu.SemaphoreType.DMA
    patch = (blocks, LANES)
    scratch = [
        vmem(forcing.shape, f32), vmem(grid, f32), vmem(grid, f32), vmem(grid, i32),
        vmem((1, slots), i32), vmem((1, slots), i32), vmem((1, blocks), i32),
        vmem(patch, i32), vmem(patch, f32), vmem(patch, f32), vmem(patch, f32),
        vmem((layers,) + patch, f32), vmem((layers,) + patch, f32),
        vmem((slots, LANES), f32), vmem((slots, LANES), i32),
        vmem((2 * LANES, 6 * LANES), bf16),
        vmem((devices, 12, LANES), f32), vmem((devices, 12, LANES), f32),
        vmem((blocks, slots), bf16), vmem((slots, blocks), bf16), vmem((grid[0], slots), bf16),
        vmem(patch, i32), vmem(patch, i32),
        vmem((3, slots, 2 * LANES), bf16), vmem((blocks, 2 * LANES), f32),
        vmem((blocks, 3 * LANES), bf16),
        vmem((devices, 8, LANES), f32), vmem((devices, 8, LANES), f32),
        vmem((3, 16, LANES), f32), vmem((8, 16, LANES), f32),
        vmem((3, 8, LANES), f32), vmem((8, 8, LANES), f32),
        dma((14,)), dma((2, 8)), dma((2, 8)), dma((2,)), dma((2,)),
    ]
    hbm = pl.BlockSpec(memory_space=pltpu.HBM)
    near = pl.BlockSpec(memory_space=pltpu.VMEM)
    arguments = (
        forcing, river_storage, river_rate, flow_code, home_slot, home_offset, listed,
        patch_cell, patch_area, canopy_water, canopy_cap, soil_water, porosity, drainage,
    )
    shapes = (soil_water.shape, patch, grid, grid, grid)
    results = pl.pallas_call(
        functools.partial(step_kernel, n_row, n_col),
        out_shape=tuple(vmem(shape, f32) for shape in shapes),
        in_specs=[hbm] * 14,
        out_specs=(near,) * 5,
        scratch_shapes=scratch,
        compiler_params=pltpu.CompilerParams(
            collective_id=0, has_side_effects=True, vmem_limit_bytes=48 * 1024 * 1024
        ),
        name="land_step",
    )(*(pltpu.with_memory_space_constraint(value, pltpu.HBM) for value in arguments))
    return pl.pallas_call(
        store_kernel,
        out_shape=tuple(jax.ShapeDtypeStruct(shape, f32) for shape in shapes),
        in_specs=[near] * 5,
        out_specs=(hbm,) * 5,
        scratch_shapes=[dma((layers + 4,))],
        compiler_params=pltpu.CompilerParams(vmem_limit_bytes=8 * 1024 * 1024),
        name="store_results",
    )(*results)


def solution(mesh):
    both = ("region", "col")
    grid = P("region", "col")
    return jax.shard_map(
        shards,
        mesh=mesh,
        in_specs=(
            P(None, "region", "col"), grid, grid, grid,
            P(both, None), P(both, None), P(both),
            P(both, None), P(both, None), P(both, None), P(both, None),
            P(None, both, None), P(None, both, None), P(None, both, None),
        ),
        out_specs=(P(None, both, None), P(both, None), grid, grid, grid),
        check_vma=False,
    )
```

```python
import functools

import jax
import jax.numpy as jnp
from jax import lax
from jax.experimental import pallas as pl
from jax.experimental.pallas import tpu as pltpu
from jax.sharding import PartitionSpec as P

ITERS = 4
LANES = 128
SPAN = 64
ORDER = 37
CHUNK = 96
QUARTERS = 4
MESH = pl.DeviceIdType.MESH
f32, bf16, i32 = jnp.float32, jnp.bfloat16, jnp.int32


def iota(shape, dim):
    return lax.broadcasted_iota(i32, shape, dim)


def lane_take(values, index):
    numbers = lax.GatherDimensionNumbers(
        offset_dims=(),
        collapsed_slice_dims=(1,),
        start_index_map=(1,),
        operand_batching_dims=(0,),
        start_indices_batching_dims=(0,),
    )
    return lax.gather(
        values,
        index[..., None],
        numbers,
        slice_sizes=(1, 1),
        mode=lax.GatherScatterMode.PROMISE_IN_BOUNDS,
    )


def split3(value):
    high = value.astype(bf16)
    rest = value - high.astype(f32)
    middle = rest.astype(bf16)
    low = (rest - middle.astype(f32)).astype(bf16)
    return high, middle, low


def hot(mask):
    return jnp.where(mask, 1.0, 0.0).astype(bf16)


def dot(lhs, rhs):
    return lax.dot_general(
        lhs, rhs, (((1,), (0,)), ((), ())), preferred_element_type=f32
    )


def dot_nt(lhs, rhs):
    return lax.dot_general(
        lhs, rhs, (((1,), (1,)), ((), ())), preferred_element_type=f32
    )


def step_shift(step, n_row, n_col):
    code = (step * ORDER) % (n_row * n_col)
    return code // n_col, code % n_col


def wanted_slots(me_r, me_c, n_row, n_col, sign, index):
    code = (lax.shift_right_logical(index, 3) * ORDER) & (n_row * n_col - 1)
    shift_r = lax.shift_right_logical(code, n_col.bit_length() - 1)
    shift_c = code & (n_col - 1)
    row = (me_r + n_row + sign * shift_r) & (n_row - 1)
    column = (me_c + n_col + sign * shift_c) & (n_col - 1)
    return (row * n_col + column) * 8 + (index & 7)


def locate_slots(wanted_at, slot, offset, rows, lanes):
    slots = slot.shape[1]
    part = 2 * LANES
    weight = jnp.where(
        iota((part, slots), 0) < LANES,
        lax.shift_right_logical(offset, 7),
        offset & (LANES - 1),
    )
    weight = weight.astype(f32).astype(bf16)
    for first in range(0, slots, part):
        wanted = wanted_at(1, iota((part, LANES), 0) + first)
        pick = jnp.concatenate(
            [hot(slot[:, l : l + LANES] == wanted) for l in range(0, slots, LANES)], axis=1
        )
        place = dot_nt(pick, weight)
        rows[first : first + part, :] = place[:, :LANES]
        lanes[first : first + part, :] = place[:, LANES:].astype(i32)


def window_weight(forcing, weight):
    grid_rows = forcing.shape[1]
    for v in range(3):
        field = forcing[v]
        below = pltpu.roll(field, grid_rows - 1, 0)
        for d, (a, b) in enumerate(zip(split3(field), split3(below))):
            at = slice(d * grid_rows, (d + 1) * grid_rows)
            weight[at, v * LANES : (v + 1) * LANES] = a
            weight[at, (3 + v) * LANES : (4 + v) * LANES] = b
    weight[3 * grid_rows :, :] = jnp.zeros((4 * LANES // 2 - 3 * grid_rows, 6 * LANES), bf16)


def cut_windows(first, grid_rows, rows, lanes, weight, windows):
    part = windows.shape[0] * 8 // QUARTERS
    lane = iota((part, LANES), 1)
    at = slice(first, first + part)
    pick = hot(rows[at, :] == (lane & (grid_rows - 1)).astype(f32))
    both = dot(jnp.concatenate([pick, pick], axis=1), weight[...])
    start = lanes[at, :]
    index = ((lane & (SPAN - 1)) + start) & (LANES - 1)
    cut = []
    for v in range(3):
        near = both[:, v * LANES : (v + 1) * LANES]
        far = both[:, (3 + v) * LANES : (4 + v) * LANES]
        cut.append(lane_take(jnp.where(lane >= start, near, far), index))
    left = lane < SPAN
    pair = jnp.where(left, cut[0], cut[1])
    last = jnp.where(left, cut[2], pltpu.roll(cut[2], part - 4, 0))
    steps = slice(first // 8, (first + part) // 8)
    windows[steps, 0:8, :] = pair.reshape(part // 8, 8, LANES)
    windows[steps, 8:12, :] = last.reshape(part // 8, 8, LANES)[:, 0:4, :]


def block_pickers(wanted_at, listed, pick_rows, pick_slots):
    blocks = listed.shape[1]
    slots = pick_slots.shape[0]
    part = 2 * LANES
    for first in range(0, slots, part):
        wanted = wanted_at(-1, iota((part, 1), 0) + first)
        pick_slots[first : first + part, :] = hot(wanted == listed)
    for first in range(0, blocks, LANES):
        size = min(LANES, blocks - first)
        column = jnp.broadcast_to(listed[:, first : first + size], (LANES, size)).T
        for l in range(0, slots, LANES):
            wanted = wanted_at(-1, iota((1, LANES), 1) + l)
            pick_rows[first : first + size, l : l + LANES] = hot(column == wanted)


def segment_tables(at, cells, last_of, run):
    cell = cells[at, :]
    lane = iota(cell.shape, 1)
    wanted = lane & (SPAN - 1)
    place = jnp.zeros_like(lane)
    for step in (64, 32, 16, 8, 4, 2, 1):
        tried = place + step
        place = jnp.where(lane_take(cell, tried) <= wanted, tried, place)
    found = lane_take(cell, place) == wanted
    last_of[at, :] = jnp.where(found, place, place + LANES)
    start = jnp.where((lane == 0) | (pltpu.roll(cell, 1, 1) != cell), lane, 0)
    for step in (1, 2, 4, 8, 16, 32, 64):
        start = jnp.maximum(start, jnp.where(lane >= step, pltpu.roll(start, step, 1), 0))
    run[at, :] = lane - start


def gather_rows(first, arrived, pick_rows, found):
    part = arrived.shape[0] * 8 // QUARTERS
    steps = slice(first // 8, (first + part) // 8)
    pair = arrived[steps, 0:8, :].reshape(part, LANES)
    half = arrived[steps, 8:12, :]
    last = jnp.concatenate([half, pltpu.roll(half, SPAN, 2)], axis=1).reshape(part, LANES)
    pick = pick_rows[:, first : first + part]
    high, middle, low = split3(jnp.concatenate([pair, last], axis=1))
    rows = dot(pick, high) + (dot(pick, middle) + dot(pick, low))
    found[...] = rows if first == 0 else found[...] + rows


def land_rows(
    at, found, cells, last_of, run, area, canopy_water, canopy_cap, canopy_out, soil, porosity, drainage, sums
):
    layers = soil.shape[0]
    cell = cells[at, :]
    lane = iota(cell.shape, 1)
    pair = found[at, :LANES]
    rainfall = lane_take(pair, cell)
    demand = lane_take(pair, cell + SPAN)
    soil_demand = lane_take(found[at, LANES:], cell)
    wetted = canopy_water[at, :] + rainfall
    cap = canopy_cap[at, :]
    flowing = jnp.maximum(wetted - cap, 0.0)
    retained = jnp.minimum(wetted, cap)
    canopy_loss = jnp.minimum(demand, retained)
    canopy_out[at, :] = retained - canopy_loss
    surface = jnp.zeros_like(flowing)
    transpired = canopy_loss
    for l in range(layers):
        filled = soil[l, at, :] + flowing
        held = jnp.minimum(filled, porosity[l, at, :])
        surface = surface + (filled - held)
        flowing = drainage[l, at, :] * held
        kept = held - flowing
        if l == 0:
            soil_loss = jnp.minimum(jnp.minimum(soil_demand, demand - canopy_loss), 0.5 * kept)
            kept = kept - soil_loss
            transpired = canopy_loss + soil_loss
        soil[l, at, :] = kept
    weight = area[at, :]
    runoff = weight * (surface + flowing)
    evap = weight * transpired
    before = run[at, :]
    for step in (1, 2, 4, 8, 16, 32, 64):
        same = before >= step
        runoff = runoff + jnp.where(same, pltpu.roll(runoff, step, 1), 0.0)
        evap = evap + jnp.where(same, pltpu.roll(evap, step, 1), 0.0)
    place = last_of[at, :]
    index = place & (LANES - 1)
    total = jnp.where(lane < SPAN, lane_take(runoff, index), lane_take(evap, index))
    total = jnp.where(place < LANES, total, 0.0)
    for d, piece in enumerate(split3(total)):
        sums[at, d * LANES : (d + 1) * LANES] = piece


def return_rows(first, pick_slots, sums, leaving):
    part = leaving.shape[0] * 8 // QUARTERS
    three = dot(pick_slots[first : first + part, :], sums[...])
    total = three[:, :LANES] + (three[:, LANES : 2 * LANES] + three[:, 2 * LANES :])
    leaving[first // 8 : (first + part) // 8, :, :] = total.reshape(part // 8, 8, LANES)


def home_picker(rows, pick_cells):
    grid_rows = pick_cells.shape[0]
    for first in range(0, rows.shape[0], LANES):
        across = rows[first : first + LANES, :].T[:grid_rows, :]
        pick_cells[:, first : first + LANES] = hot(
            across == iota((grid_rows, LANES), 0).astype(f32)
        )


def place_sums(first, back, lanes, pick_cells):
    part = back.shape[0] * 8 // QUARTERS
    lane = iota((part, LANES), 1)
    at = slice(first, first + part)
    sent = back[first // 8 : (first + part) // 8, :, :].reshape(part, LANES)
    start = lanes[at, :]
    index = (lane - start) & (LANES - 1)
    inside = index < SPAN
    near = inside & (lane >= start)
    far = inside & (lane < start)
    runoff = lane_take(sent, index)
    evap = lane_take(sent, (index + SPAN) & (LANES - 1))
    spread = jnp.concatenate(
        [
            jnp.where(near, runoff, 0.0),
            jnp.where(near, evap, 0.0),
            jnp.where(far, runoff, 0.0),
            jnp.where(far, evap, 0.0),
        ],
        axis=1,
    )
    high, middle, low = split3(spread)
    pick = pick_cells[:, at]
    return dot(pick, high) + (dot(pick, middle) + dot(pick, low))


def cell_sums(total):
    first_row = iota((total.shape[0], 2 * LANES), 0) == 0
    carried = pltpu.roll(total[:, 2 * LANES :], 1, 0)
    total = total[:, : 2 * LANES] + jnp.where(first_row, 0.0, carried)
    return total[:, :LANES], total[:, LANES:]


def pack_edges(field):
    lane = iota((8, LANES), 1)
    packed = jnp.zeros((8, LANES), field.dtype)
    for i in range(field.shape[0] // 8):
        piece = field[8 * i : 8 * i + 8, :]
        first = pltpu.roll(piece, 4 * i, 1) if i else piece
        last = pltpu.roll(piece, (SPAN + 4 * i + 4) % LANES, 1)
        packed = jnp.where((lane >= 4 * i) & (lane < 4 * i + 4), first, packed)
        packed = jnp.where((lane >= SPAN + 4 * i) & (lane < SPAN + 4 * i + 4), last, packed)
    return packed


def extend(field, halo, inside):
    up, down, left, right = inside
    lane = iota((8, LANES), 1)
    on_right = (lane < 4) & right
    on_left = (lane >= LANES - 4) & left

    def side(from_right, from_left):
        return jnp.where(on_right, from_right, jnp.where(on_left, from_left, 0.0))

    centre = jnp.concatenate(
        [jnp.where(up, halo[0], 0.0), field, jnp.where(down, halo[1], 0.0)], axis=0
    )
    sides = [jnp.where(up, side(halo[5], halo[4]), 0.0)]
    for i in range(field.shape[0] // 8):
        from_right = pltpu.roll(halo[3], LANES - 4 * i, 1) if i else halo[3]
        from_left = pltpu.roll(halo[2], LANES - 4 - (SPAN + 4 * i), 1) if 4 * i < SPAN - 4 else halo[2]
        sides.append(side(from_right, from_left))
    sides.append(jnp.where(down, side(halo[7], halo[6]), 0.0))
    return centre, jnp.concatenate(sides, axis=0)


def route(storage, rate, code):
    height = storage[0].shape[0]
    lane = iota(storage[0].shape, 1)

    def across(pair, east):
        centre, side = (pltpu.roll(x, 1 if east else LANES - 1, 1) for x in pair)
        edge = lane == (0 if east else LANES - 1)
        return jnp.where(edge, side, centre), jnp.where(edge, centre, side)

    def inflow(outflow):
        def from_row(step, column):
            bits = {
                (0, 1): 1, (1, 1): 2, (1, 0): 4, (1, -1): 8,
                (0, -1): 16, (-1, -1): 32, (-1, 0): 64, (-1, 1): 128,
            }
            if (step, column) == (0, 0):
                return None
            bit = float(bits[step, column])
            return [jnp.where(c == bit, o, 0.0) for c, o in zip(code, outflow)]

        total = None
        for column in (1, 0, -1):
            gathered = None
            for step in (1, -1, 0):
                moved = from_row(step, column)
                if moved is None:
                    continue
                if step:
                    moved = [pltpu.roll(x, 1 if step > 0 else height - 1, 0) for x in moved]
                gathered = moved if gathered is None else [a + b for a, b in zip(gathered, moved)]
            if column:
                gathered = across(gathered, column > 0)
            total = list(gathered) if total is None else [a + b for a, b in zip(total, gathered)]
        return total

    for _ in range(ITERS):
        outflow = [a * b for a, b in zip(rate, storage)]
        storage = [s - o + n for s, o, n in zip(storage, outflow, inflow(outflow))]
    return storage[0]


def step_kernel(
    n_row,
    n_col,
    forcing_h, storage_h, rate_h, code_h, slot_h, offset_h, list_h,
    cell_h, area_h, water_h, cap_h, soil_h, porosity_h, drainage_h,
    soil, canopy, runoff_o, evap_o, river_o,
    forcing, storage, rate, code, slot, offset, listed,
    cells, area, water, cap, porosity, drainage,
    rows, lanes, weight, windows, arrived, pick_rows, pick_slots, pick_cells,
    last_of, run, found, sums, leaving, back,
    fixed_edge, fixed_halo, edge, halo,
    load_sem, fixed_sem, edge_sem, out_sem, back_sem, arrive_sem, return_sem, ready,
):
    me_r, me_c = lax.axis_index("region"), lax.axis_index("col")
    devices = n_row * n_col
    steps = devices // QUARTERS
    quarter = steps * 8
    wanted_at = functools.partial(wanted_slots, me_r, me_c, n_row, n_col)

    def peer(step, sign):
        shift_r, shift_c = step_shift(step, n_row, n_col)
        if sign > 0:
            return (me_r + shift_r) % n_row, (me_c + shift_c) % n_col
        return (me_r + n_row - shift_r) % n_row, (me_c + n_col - shift_c) % n_col

    barrier = pltpu.get_barrier_semaphore()
    row_peers = [(me_r, (me_c + i) % n_col) for i in range(1, n_col)]
    column_peers = [((me_r + i) % n_row, me_c) for i in range(1, n_row)]
    for to in row_peers + column_peers:
        pl.semaphore_signal(barrier, inc=1, device_id=to, device_id_type=MESH)

    loads = [
        (slot_h, slot), (offset_h, offset), (forcing_h, forcing), (rate_h, rate), (code_h, code),
        (list_h, listed), (cell_h, cells), (storage_h, storage), (area_h, area),
        (water_h, water), (cap_h, cap), (soil_h, soil), (porosity_h, porosity), (drainage_h, drainage),
    ]
    loads = [pltpu.make_async_copy(a, b, load_sem.at[i]) for i, (a, b) in enumerate(loads)]
    for copy in loads:
        copy.start()
    for copy in loads[:3]:
        copy.wait()
    locate_slots(wanted_at, slot[...], offset[...], rows, lanes)
    pl.semaphore_wait(barrier, n_row + n_col - 2)
    for to in column_peers:
        pl.semaphore_signal(ready, inc=1, device_id=to, device_id_type=MESH)
    height = forcing.shape[1]
    window_weight(forcing, weight)

    def send_out(part, step, carry):
        pltpu.make_async_remote_copy(
            src_ref=windows.at[step], dst_ref=arrived.at[step],
            send_sem=out_sem.at[0], recv_sem=arrive_sem.at[part],
            device_id=peer(step, 1), device_id_type=MESH,
        ).start()
        return carry

    def span(part):
        first = part * steps if part else 1
        return first, (part + 1) * steps

    for part in range(QUARTERS):
        cut_windows(part * quarter, height, rows, lanes, weight, windows)
        if part == 0:
            pl.semaphore_wait(ready, n_row - 1)
        lax.fori_loop(*span(part), functools.partial(send_out, part), 0)
    arrived[0] = windows[0]

    routes = [
        (2, (1, 0)), (1, (-1, 0)), (0, (0, 1)), (0, (0, -1)),
        (2, (1, 1)), (2, (1, -1)), (1, (-1, 1)), (1, (-1, -1)),
    ]
    row_in = {-1: me_r > 0, 1: me_r < n_row - 1}
    column_in = {-1: me_c > 0, 1: me_c < n_col - 1}

    def has(down, right):
        if down and right:
            return row_in[down] & column_in[right]
        return row_in[down] if down else column_in[right]

    def edge_copies(source, target, sems):
        return [
            pltpu.make_async_remote_copy(
                src_ref=source.at[which], dst_ref=target.at[i],
                send_sem=sems.at[0, i], recv_sem=sems.at[1, i],
                device_id=((me_r + n_row + down) % n_row, (me_c + n_col + right) % n_col),
                device_id_type=MESH,
            )
            for i, (which, (down, right)) in enumerate(routes)
        ]

    def start_edges(copies):
        for copy, (_, (down, right)) in zip(copies, routes):
            pl.when(has(down, right))(copy.start)

    def wait_edges(copies):
        for copy, (_, (down, right)) in zip(copies, routes):
            pl.when(has(down, right))(copy.wait_send)
            pl.when(has(-down, -right))(copy.wait_recv)

    loads[3].wait()
    loads[4].wait()
    for first, field in ((0, rate[...]), (8, code[...].astype(f32))):
        at = slice(first, first + 8)
        fixed_edge[0, at, :] = pack_edges(field)
        fixed_edge[1, at, :] = field[:8, :]
        fixed_edge[2, at, :] = field[height - 8 :, :]
    fixed_copies = edge_copies(fixed_edge, fixed_halo, fixed_sem)
    start_edges(fixed_copies)

    loads[5].wait()
    block_pickers(wanted_at, listed[...], pick_rows, pick_slots)
    home_picker(rows, pick_cells)
    loads[6].wait()
    blocks = cells.shape[0]

    def chunk(i):
        return pl.ds(pl.multiple_of(i * CHUNK, CHUNK), CHUNK)

    def tables(i, carry):
        segment_tables(chunk(i), cells, last_of, run)
        return carry

    lax.fori_loop(0, blocks // CHUNK, tables, 0)
    for copy in loads[7:]:
        copy.wait()

    def wait_bytes(buffer, first, last, sem):
        block = buffer.at[pl.ds(first, last - first)]
        pltpu.make_async_copy(block, block, sem).wait()

    for part in range(QUARTERS):
        wait_bytes(arrived, *span(part), arrive_sem.at[part])
        gather_rows(part * quarter, arrived, pick_rows, found)

    def land(i, carry):
        land_rows(
            chunk(i), found, cells, last_of, run, area, water, cap, canopy, soil, porosity, drainage, sums
        )
        return carry

    lax.fori_loop(0, blocks // CHUNK, land, 0)

    def send_back(part, step, carry):
        pltpu.make_async_remote_copy(
            src_ref=leaving.at[step], dst_ref=back.at[step],
            send_sem=back_sem.at[0], recv_sem=return_sem.at[part],
            device_id=peer(step, -1), device_id_type=MESH,
        ).start()
        return carry

    for part in range(QUARTERS):
        return_rows(part * quarter, pick_slots, sums, leaving)
        lax.fori_loop(*span(part), functools.partial(send_back, part), 0)
    back[0] = leaving[0]
    wait_edges(fixed_copies)
    inside = (row_in[-1], row_in[1], column_in[-1], column_in[1])
    for i, field in ((1, rate[...]), (2, code[...].astype(f32))):
        at = slice(8 * (i - 1), 8 * i)
        river_o[2 * i], river_o[2 * i + 1] = extend(
            field, [fixed_halo[j, at, :] for j in range(8)], inside
        )
    wait_bytes(windows, 1, devices, out_sem.at[0])

    total = None
    for part in range(QUARTERS):
        wait_bytes(back, *span(part), return_sem.at[part])
        added = place_sums(part * quarter, back, lanes, pick_cells)
        total = added if total is None else total + added
    cell_runoff, cell_evap = cell_sums(total)
    river = storage[...] + cell_runoff
    edge[0] = pack_edges(river)
    edge[1] = river[:8, :]
    edge[2] = river[height - 8 :, :]
    edge_sent = edge_copies(edge, halo, edge_sem)
    start_edges(edge_sent)
    runoff_o[...] = cell_runoff
    evap_o[...] = cell_evap
    wait_bytes(leaving, 1, devices, back_sem.at[0])
    wait_edges(edge_sent)
    river_o[0], river_o[1] = extend(river, [halo[i] for i in range(8)], inside)


def store_kernel(soil, canopy, runoff, evap, tiles, soil_o, canopy_o, runoff_o, evap_o, river_o, river, sems):
    pairs = [(soil.at[l], soil_o.at[l]) for l in range(soil.shape[0])]
    pairs += [(canopy, canopy_o), (runoff, runoff_o), (evap, evap_o)]
    copies = [pltpu.make_async_copy(a, b, sems.at[i]) for i, (a, b) in enumerate(pairs)]
    for copy in copies:
        copy.start()
    final = route((tiles[0], tiles[1]), (tiles[2], tiles[3]), (tiles[4], tiles[5]))
    river[...] = final[8 : 8 + river.shape[0], :]
    last = pltpu.make_async_copy(river, river_o, sems.at[len(pairs)])
    last.start()
    for copy in copies:
        copy.wait()
    last.wait()


def shards(
    forcing, river_storage, river_rate, flow_code, home_slot, home_offset, worker_list,
    patch_cell, patch_area, canopy_water, canopy_cap, soil_water, porosity, drainage,
):
    n_row, n_col = lax.axis_size("region"), lax.axis_size("col")
    devices = n_row * n_col
    grid = river_storage.shape
    slots = home_slot.shape[1]
    blocks = patch_cell.shape[0]
    layers = soil_water.shape[0]
    listed = worker_list.reshape(1, blocks)
    vmem = pltpu.VMEM
    dma = pltpu.SemaphoreType.DMA
    patch = (blocks, LANES)
    scratch = [
        vmem(forcing.shape, f32), vmem(grid, f32), vmem(grid, f32), vmem(grid, i32),
        vmem((1, slots), i32), vmem((1, slots), i32), vmem((1, blocks), i32),
        vmem(patch, i32), vmem(patch, f32), vmem(patch, f32), vmem(patch, f32),
        vmem((layers,) + patch, f32), vmem((layers,) + patch, f32),
        vmem((slots, LANES), f32), vmem((slots, LANES), i32),
        vmem((2 * LANES, 6 * LANES), bf16),
        vmem((devices, 12, LANES), f32), vmem((devices, 12, LANES), f32),
        vmem((blocks, slots), bf16), vmem((slots, blocks), bf16), vmem((grid[0], slots), bf16),
        vmem(patch, i32), vmem(patch, i32),
        vmem((blocks, 2 * LANES), f32),
        vmem((blocks, 3 * LANES), bf16),
        vmem((devices, 8, LANES), f32), vmem((devices, 8, LANES), f32),
        vmem((3, 16, LANES), f32), vmem((8, 16, LANES), f32),
        vmem((3, 8, LANES), f32), vmem((8, 8, LANES), f32),
        dma((14,)), dma((2, 8)), dma((2, 8)), dma((1,)), dma((1,)),
        dma((QUARTERS,)), dma((QUARTERS,)), pltpu.SemaphoreType.REGULAR,
    ]
    hbm = pl.BlockSpec(memory_space=pltpu.HBM)
    near = pl.BlockSpec(memory_space=pltpu.VMEM)
    arguments = (
        forcing, river_storage, river_rate, flow_code, home_slot, home_offset, listed,
        patch_cell, patch_area, canopy_water, canopy_cap, soil_water, porosity, drainage,
    )
    shapes = (soil_water.shape, patch, grid, grid, grid)
    results = pl.pallas_call(
        functools.partial(step_kernel, n_row, n_col),
        out_shape=tuple(vmem(shape, f32) for shape in shapes[:4] + ((6, grid[0] + 16, LANES),)),
        in_specs=[hbm] * 14,
        out_specs=(near,) * 5,
        scratch_shapes=scratch,
        compiler_params=pltpu.CompilerParams(
            collective_id=0, has_side_effects=True, vmem_limit_bytes=48 * 1024 * 1024
        ),
        name="land_step",
    )(*(pltpu.with_memory_space_constraint(value, pltpu.HBM) for value in arguments))
    return pl.pallas_call(
        store_kernel,
        out_shape=tuple(jax.ShapeDtypeStruct(shape, f32) for shape in shapes),
        in_specs=[near] * 5,
        out_specs=(hbm,) * 5,
        scratch_shapes=[vmem(grid, f32), dma((layers + 4,))],
        compiler_params=pltpu.CompilerParams(vmem_limit_bytes=8 * 1024 * 1024),
        name="store_results",
    )(*results)


def solution(mesh):
    both = ("region", "col")
    grid = P("region", "col")
    return jax.shard_map(
        shards,
        mesh=mesh,
        in_specs=(
            P(None, "region", "col"), grid, grid, grid,
            P(both, None), P(both, None), P(both),
            P(both, None), P(both, None), P(both, None), P(both, None),
            P(None, both, None), P(None, both, None), P(None, both, None),
        ),
        out_specs=(P(None, both, None), P(both, None), grid, grid, grid),
        check_vma=False,
    )
```
